32 devices in a mesh: groups: 2 (over x), expert: 16 (over z, y, core).
Axes of the slice: x: 2, y: 2, z: 4, core: 2. Of those that a mesh axis runs over, the one named last changes fastest.
Arguments:
- tokens: bfloat16 [384, 3584], P(('groups', 'expert')), parts along dimension 0, may hold values from -6 to 6
- expert_ids: int32 [384, 8], P(('groups', 'expert')), parts along dimension 0, may hold values from 0 to 15, all different within a row; in each aligned block of 12 rows (0 to 11, 12 to 23, ...) at most 8 rows name the same one
- gate_weights: float32 [384, 8], P(('groups', 'expert')), parts along dimension 0, may hold values from 0.1 to 1
- w_gate: bfloat16 [16, 3584, 2048], P('expert'), may hold values from -0.09375 to 0.09375
- w_up: bfloat16 [16, 3584, 2048], P('expert'), may hold values from -0.09375 to 0.09375
- w_down: bfloat16 [16, 2048, 3584], P('expert'), may hold values from -0.125 to 0.125
Outputs:
- moe_out: bfloat16 [384, 3584], P(('groups', 'expert')), parts along dimension 0
The draws below stay inside these ranges and needn't reach their ends.
There are 2 independent parts, one for each index of `groups`. The reference program is written for one: setup_inputs(seed, part) draws one part's arguments, and reference() takes and returns one part's arrays. A program takes and returns all parts, laid end to end along the dimension named above; an argument that names none is the same for every part. Nothing has to cross between parts.
Inputs may be any that keep to these rules, and one draw needn't show every extreme that they name: `expert_ids`: each row names 8 different experts. Within the rows of one block (one device's 12 tokens) no expert is named more than 8 times, and in every draw some expert is named exactly 8 times in some block.
All inputs are finite; a program needn't handle non-finite values.
Results may differ from the reference program's by a relative error of at most 0.005.
Values may be sent and summed in bfloat16 or wider, within the bound.
A program may use at most 128 MiB of HBM per device.

```python
import math
import jax
import jax.numpy as jnp
import numpy as np
from jax import lax

D = 3584
FFE = 2048
EXPERTS = 16
TOP = 8
TOK_DEV = 12
CAP = 8
SHARDS = 1
TOKENS = 192
N_EXPERT = 16


def block_levels(key, extent, cuts, low, largest):
    level, own = 1.0, jax.random.fold_in(key, 6)
    for axis_at, shards_of in cuts:
        draws = jnp.exp(jax.random.uniform(jax.random.fold_in(own, axis_at), (shards_of,), jnp.float32, low / len(cuts), largest / len(cuts)))
        level = level * jnp.repeat(draws, extent[axis_at] // shards_of).reshape([-1 if axis == axis_at else 1 for axis in range(len(extent))])
    return level


def deal_out(stream_key, own, number, rows, count, top, most, lean):
    order = jax.random.permutation(stream_key, count)
    packed, common = load_shares(count, rows * top, most, lean, True), load_shares(count, rows * top, most, lean, False)
    places = jnp.arange(count)

    def named(sizes, turn):
        used = int((sizes > 0).sum())
        fixed = max(1, used // 4)
        passed = fixed + (places - fixed + turn * (used - fixed)) % max(1, count - fixed)
        return jnp.zeros((count,), jnp.int32).at[order[jnp.where(places < fixed, places, passed)]].set(jnp.asarray(sizes, jnp.int32))

    sizes = jnp.where(number % 4 == 0, named(packed, number // 4), named(common, number - number // 4 - 1))
    mixed = jax.random.permutation(jax.random.fold_in(own, 3), count)
    giver, taker = mixed[0:count // 2 * 2:2], mixed[1:count // 2 * 2:2]
    room = jnp.minimum(sizes[giver] - 1, most - sizes[taker]) // 2
    room = jnp.where((giver == order[0]) | (taker == order[0]) | (sizes[taker] == 0), 0, jnp.maximum(room, 0))
    passed = jax.random.randint(jax.random.fold_in(own, 4), (count // 2,), 0, 1 << 20) % (room + 1)
    sizes = sizes.at[giver].add(-passed).at[taker].add(passed)
    labels = jnp.searchsorted(jnp.cumsum(sizes), jnp.arange(rows * top), side="right").astype(jnp.int32)
    grid = labels.reshape(top, rows).T
    grid = grid[jax.random.permutation(jax.random.fold_in(own, 1), rows)]
    turn = jax.random.randint(jax.random.fold_in(own, 2), (rows, 1), 0, top)
    return jnp.take_along_axis(grid, (jnp.arange(top)[None, :] + turn) % top, axis=1)


def load_shares(number_of, total, reach, slope, full):
    portions = [(1 << 20) // math.isqrt(rank ** slope) + 1 for rank in range(1, number_of + 1)]
    largest = reach if full else min(reach, max(-(-total // number_of), total * portions[0] // sum(portions)))
    least = 1 if total - largest >= number_of - 1 else 0
    given, rest = [largest] + [least] * (number_of - 1), total - largest - least * (number_of - 1)
    while rest > 0:
        candidates = [i for i in range(1, number_of) if given[i] < largest] or [i for i in range(1, number_of) if given[i] < reach]
        whole, remaining = sum([portions[i] for i in candidates]), rest
        for i in candidates:
            addition = min(reach - given[i], max(1, remaining * portions[i] // whole), rest)
            given[i] = given[i] + addition
            rest = rest - addition
    return np.array(given)


def centred(rng, shape, spread, reach, split=(), kind=jnp.bfloat16):
    entries = jax.random.normal(rng, shape, jnp.float32) * spread
    if len(split) > 0:
        entries = block_levels(rng, shape, split, -0.22, 0.18) * entries
    return jnp.clip(entries, min=-reach, max=reach).astype(kind)


def setup_inputs(seed: int = 0, part: int = 0) -> dict:
    keys = jax.random.split(jax.random.key(seed), 7)
    part_splits = jax.random.split(jax.random.fold_in(keys[6], part), 7)
    tokens = centred(part_splits[0], (TOKENS, D), 1.0, 6.0, ((0, 16),))
    expert_ids_keys = jax.random.split(jax.random.fold_in(part_splits[1], 1), TOKENS // TOK_DEV)
    expert_ids_turns = jax.random.permutation(jax.random.fold_in(part_splits[1], 3), TOKENS // TOK_DEV)
    expert_ids = jax.vmap(lambda own, number: deal_out(jax.random.fold_in(part_splits[1], 2), own, number, TOK_DEV, EXPERTS, TOP, CAP, 2))(expert_ids_keys, expert_ids_turns).reshape((TOKENS, TOP))
    gate_weights = jnp.clip(jnp.exp(math.log(1.0) - 2.3025851 * jax.random.uniform(part_splits[2], (TOKENS, TOP), jnp.float32) ** block_levels(part_splits[2], (TOKENS, TOP), ((0, 16),), -0.2, 0.2)), 0.1, 1.0)
    w_gate = centred(keys[3], (EXPERTS * SHARDS, D, FFE // SHARDS), D ** -0.5, 0.09375, ((0, 16),))
    w_up = centred(keys[4], (EXPERTS * SHARDS, D, FFE // SHARDS), D ** -0.5, 0.09375, ((0, 16),))
    w_down = centred(keys[5], (EXPERTS * SHARDS, FFE // SHARDS, D), FFE ** -0.5, 0.125, ((0, 16),))
    return dict(tokens=tokens, expert_ids=expert_ids, gate_weights=gate_weights, w_gate=w_gate, w_up=w_up, w_down=w_down)


def slot_numbers(routed):
    chosen = (routed[..., None] == jnp.arange(EXPERTS, dtype=jnp.int32)).astype(jnp.int32)
    counts = jnp.sum(chosen, axis=2)
    before = jnp.cumsum(counts, axis=1) - counts
    return jnp.sum(chosen * before[:, :, None, :], axis=3)


def reference(tokens, expert_ids, gate_weights, w_gate, w_up, w_down):
    shards = N_EXPERT // EXPERTS
    slice_units = FFE // shards
    slot_index = slot_numbers(expert_ids.reshape(N_EXPERT, TOK_DEV, TOP)).reshape(TOKENS, TOP)
    block_of = (jnp.arange(TOKENS, dtype=jnp.int32) // TOK_DEV).astype(jnp.int32)
    gate_all = w_gate.reshape(shards, EXPERTS, D, slice_units)
    up_all = w_up.reshape(shards, EXPERTS, D, slice_units)
    down_all = w_down.reshape(shards, EXPERTS, slice_units, D)
    buffer_rows = N_EXPERT * CAP

    def one_expert(running, expert):
        chosen = expert_ids == expert
        is_used = jnp.any(chosen, axis=1)
        slot_e = jnp.sum(jnp.where(chosen, slot_index, 0), axis=1).astype(jnp.int32)
        target = jnp.where(is_used, block_of * CAP + slot_e, buffer_rows).astype(jnp.int32)
        buffer = jnp.zeros((buffer_rows, D), jnp.bfloat16).at[target].set(tokens, mode="drop")
        gate_full = jnp.transpose(gate_all[:, expert], (1, 0, 2)).reshape(D, FFE)
        up_full = jnp.transpose(up_all[:, expert], (1, 0, 2)).reshape(D, FFE)
        down_full = down_all[:, expert].reshape(FFE, D)
        gate_act = jnp.dot(buffer, gate_full, preferred_element_type=jnp.float32)
        up_act = jnp.dot(buffer, up_full, preferred_element_type=jnp.float32)
        hidden = (jax.nn.silu(gate_act) * up_act).astype(jnp.bfloat16)
        expert_rows = jnp.dot(hidden, down_full, preferred_element_type=jnp.float32)
        weight = jnp.sum(jnp.where(chosen, gate_weights, jnp.zeros_like(gate_weights)), axis=1)
        picked = expert_rows[jnp.minimum(target, buffer_rows - 1)] * weight[:, None]
        return running + picked, None

    summed_all, _ = lax.scan(one_expert, jnp.zeros((TOKENS, D), jnp.float32), jnp.arange(EXPERTS, dtype=jnp.int32))
    return summed_all.astype(jnp.bfloat16)
```

```python
import functools

import jax
import jax.numpy as jnp
from jax import lax
from jax.experimental import pallas as pl
from jax.experimental.pallas import tpu as pltpu
from jax.sharding import PartitionSpec as P

EXPERTS = 16
CAP = 8
TILE = 16
LANES = 128
UNITS = 256


def kernel(
    n,
    tok_ref,
    ids_ref,
    gw_ref,
    wg_hbm,
    wu_hbm,
    wd_hbm,
    out_ref,
    gathered,
    wg,
    wu,
    wd,
    rows_in,
    hidden,
    tail_out,
    kept,
    sending,
    landed,
    wsem,
    dsem,
    ag_send,
    ag_recv,
    rs_send,
    rs_recv,
):
    rows, width = tok_ref.shape
    pad = TILE - rows
    parts = rows // pad
    sec = width // (parts + 1)
    packed = parts * sec
    units = wg.shape[1]
    slots = n * CAP
    stages = n.bit_length() - 1
    me = lax.axis_index("expert")

    def partner(bit):
        return me + bit - 2 * bit * ((me // bit) % 2)

    def weight_copies(j):
        cols = pl.ds(j * UNITS, UNITS)
        return (
            pltpu.make_async_copy(wg_hbm.at[0, :, cols], wg.at[:, cols], wsem.at[0, j]),
            pltpu.make_async_copy(wu_hbm.at[0, :, cols], wu.at[:, cols], wsem.at[1, j]),
        )

    def down_copy(s):
        cols = pl.ds(s * sec, sec)
        return pltpu.make_async_copy(wd_hbm.at[0, :, cols], wd.at[:, cols], dsem.at[s])

    barrier = pltpu.get_barrier_semaphore()
    for k in range(stages):
        pl.semaphore_signal(barrier, inc=1, device_id={"expert": partner(1 << k)})

    for j in range(units // UNITS):
        for copy in weight_copies(j):
            copy.start()
    for s in [parts] + list(range(parts)):
        down_copy(s).start()

    lane = lax.broadcasted_iota(jnp.int32, (rows, LANES), 1)
    row = lax.broadcasted_iota(jnp.int32, (rows, LANES), 0)
    weight = jnp.zeros((rows, LANES), jnp.float32)
    for j in range(ids_ref.shape[1]):
        weight = weight + jnp.where(
            ids_ref[:, j : j + 1] == lane % EXPERTS, gw_ref[:, j : j + 1], 0.0
        )
    chosen = jnp.where(weight > 0.0, 1.0, 0.0)
    slot = jnp.zeros((rows, LANES), jnp.float32)
    for t in range(rows - 1):
        slot = slot + jnp.where(row > t, chosen[t : t + 1, :], 0.0)
    first = weight.astype(jnp.bfloat16).astype(jnp.float32)
    second = (weight - first).astype(jnp.bfloat16).astype(jnp.float32)
    third = weight - first - second
    kind = lane // EXPERTS
    route = jnp.where(
        kind == 0,
        slot,
        jnp.where(kind == 1, first, jnp.where(kind == 2, second, jnp.where(kind == 3, third, 0.0))),
    )
    gathered[0:TILE, packed:] = jnp.concatenate(
        [route, jnp.zeros((pad, LANES), jnp.float32)], axis=0
    ).astype(jnp.bfloat16)
    mine = tok_ref[...].astype(jnp.float32)
    for s in range(parts):
        gathered[0:TILE, s * sec : (s + 1) * sec] = jnp.concatenate(
            [mine[:, s * sec : (s + 1) * sec], mine[pad * s : pad * (s + 1), packed:]], axis=0
        ).astype(jnp.bfloat16)

    pl.semaphore_wait(barrier, stages)

    def block(i):
        return gathered.at[pl.ds(i * TILE, TILE), :]

    def gather_copy(k, i):
        to = (1 << k) + i
        return pltpu.make_async_remote_copy(
            src_ref=block(i),
            dst_ref=block(to),
            send_sem=ag_send.at[to],
            recv_sem=ag_recv.at[to],
            device_id={"expert": partner(n >> (k + 1))},
            device_id_type=pl.DeviceIdType.MESH,
        )

    for k in range(stages):
        gather_copy(k, 0).start()
    order = sorted(range(1, n), key=lambda i: (i >= n // 2, bin(i).count("1"), i))
    for i in order:
        k0 = i.bit_length() - 1
        gather_copy(k0, i - (1 << k0)).wait_recv()
        for k in range(k0 + 1, stages):
            gather_copy(k, i).start()

    expert = me % EXPERTS
    all_rows = n * TILE
    lanes = lax.broadcasted_iota(jnp.int32, (all_rows, LANES), 1)
    table = gathered[:, packed:].astype(jnp.float32)
    slot_of = jnp.sum(jnp.where(lanes == expert, table, 0.0), axis=1, keepdims=True)
    weight_of = jnp.sum(
        jnp.where((lanes % EXPERTS == expert) & (lanes >= EXPERTS), table, 0.0),
        axis=1,
        keepdims=True,
    )
    r_at = lax.broadcasted_iota(jnp.int32, (all_rows, slots), 0)
    m_at = lax.broadcasted_iota(jnp.int32, (all_rows, slots), 1)
    mixing = jnp.where(
        (r_at // TILE == m_at // CAP) & (slot_of == (m_at % CAP).astype(jnp.float32)),
        weight_of,
        0.0,
    )
    mixing_t = mixing.T
    slot_weight = jnp.sum(mixing_t, axis=1, keepdims=True)
    place = jnp.where(mixing > 0.0, 1.0, 0.0)
    pick = jnp.where(mixing_t > 0.0, 1.0, 0.0)
    spare = r_at % TILE >= rows
    spare_t = lax.broadcasted_iota(jnp.int32, (slots, all_rows), 1) % TILE >= rows
    place_main = place.astype(jnp.bfloat16)
    pick_main = pick.astype(jnp.bfloat16)

    tail = jnp.zeros((slots, sec), jnp.float32)
    for s in range(parts):
        data = gathered[:, s * sec : (s + 1) * sec]
        rows_in[:, s * sec : (s + 1) * sec] = jnp.dot(
            pick_main, data, preferred_element_type=jnp.float32
        ).astype(jnp.bfloat16)
        pick_tail = jnp.where(spare_t, pltpu.roll(pick, rows - pad * s, 1), 0.0)
        tail = tail + jnp.dot(
            pick_tail.astype(jnp.bfloat16), data, preferred_element_type=jnp.float32
        )
    rows_in[:, packed:] = tail.astype(jnp.bfloat16)

    @pl.loop(0, units // UNITS)
    def _(j):
        for copy in weight_copies(j):
            copy.wait()
        cols = pl.ds(pl.multiple_of(j * UNITS, UNITS), UNITS)
        gate = jnp.dot(rows_in[...], wg[:, cols], preferred_element_type=jnp.float32)
        up = jnp.dot(rows_in[...], wu[:, cols], preferred_element_type=jnp.float32)
        hidden[:, cols] = (gate / (1.0 + jnp.exp(-gate)) * up).astype(jnp.bfloat16)

    def down(s):
        down_copy(s).wait()
        result = jnp.dot(
            hidden[...], wd[:, s * sec : (s + 1) * sec], preferred_element_type=jnp.float32
        )
        return (result * slot_weight).astype(jnp.bfloat16)

    def sum_copy(s, t):
        half = all_rows >> (t + 1)
        span = pl.ds(half, half)
        return pltpu.make_async_remote_copy(
            src_ref=sending.at[s, span, :],
            dst_ref=landed.at[s, span, :],
            send_sem=rs_send.at[s, t],
            recv_sem=rs_recv.at[s, t],
            device_id={"expert": partner(1 << t)},
            device_id_type=pl.DeviceIdType.MESH,
        )

    def first_stage(s):
        here = down(s)
        place_tail = jnp.where(spare, pltpu.roll(place, rows - pad * s, 0), 0.0)
        half = all_rows // 2
        total = jnp.dot(place_main, here, preferred_element_type=jnp.float32) + jnp.dot(
            place_tail.astype(jnp.bfloat16), tail_out[...], preferred_element_type=jnp.float32
        )
        sending[s, half:, :] = total[half:].astype(jnp.bfloat16)
        sum_copy(s, 0).start()
        kept[s] = total[:half]

    def later_stage(s, t):
        sum_copy(s, t - 1).wait_recv()
        half = all_rows >> (t + 1)
        total = kept[s, : 2 * half, :] + landed[s, 2 * half : 4 * half, :].astype(jnp.float32)
        sending[s, half : 2 * half, :] = total[half:].astype(jnp.bfloat16)
        sum_copy(s, t).start()
        kept[s, :half, :] = total[:half]

    def last_stage(s):
        sum_copy(s, stages - 1).wait_recv()
        return kept[s, :TILE, :] + landed[s, TILE : 2 * TILE, :].astype(jnp.float32)

    tail_out[...] = down(parts)
    tails = []
    for step in range(parts + stages):
        for s in range(parts):
            t = step - s
            if t == 0:
                first_stage(s)
        for s in range(parts):
            t = step - s
            if 0 < t < stages:
                later_stage(s, t)
            elif t == stages:
                done = last_stage(s)
                out_ref[:, s * sec : (s + 1) * sec] = done[:rows].astype(jnp.bfloat16)
                tails.append(done[rows:])
    out_ref[:, packed:] = jnp.concatenate(tails, axis=0).astype(jnp.bfloat16)

    for k in range(stages):
        for i in range(1 << k):
            gather_copy(k, i).wait_send()
    for s in range(parts):
        for t in range(stages):
            sum_copy(s, t).wait_send()


def body(tokens, expert_ids, gate_weights, w_gate, w_up, w_down):
    n = lax.axis_size("expert")
    rows, width = tokens.shape
    units = w_gate.shape[2]
    pad = TILE - rows
    parts = rows // pad
    sec = width // (parts + 1)
    stages = n.bit_length() - 1
    vmem = pl.BlockSpec(memory_space=pltpu.VMEM)
    hbm = pl.BlockSpec(memory_space=pl.ANY)
    return pl.pallas_call(
        functools.partial(kernel, n),
        out_shape=jax.ShapeDtypeStruct((rows, width), jnp.bfloat16),
        in_specs=[vmem, vmem, vmem, hbm, hbm, hbm],
        out_specs=vmem,
        scratch_shapes=[
            pltpu.VMEM((n * TILE, parts * sec + LANES), jnp.bfloat16),
            pltpu.VMEM((width, units), jnp.bfloat16),
            pltpu.VMEM((width, units), jnp.bfloat16),
            pltpu.VMEM((units, width), jnp.bfloat16),
            pltpu.VMEM((n * CAP, width), jnp.bfloat16),
            pltpu.VMEM((n * CAP, units), jnp.bfloat16),
            pltpu.VMEM((n * CAP, sec), jnp.bfloat16),
            pltpu.VMEM((parts, n * TILE // 2, sec), jnp.float32),
            pltpu.VMEM((parts, n * TILE, sec), jnp.bfloat16),
            pltpu.VMEM((parts, n * TILE, sec), jnp.bfloat16),
            pltpu.SemaphoreType.DMA((2, units // UNITS)),
            pltpu.SemaphoreType.DMA((parts + 1,)),
            pltpu.SemaphoreType.DMA((n,)),
            pltpu.SemaphoreType.DMA((n,)),
            pltpu.SemaphoreType.DMA((parts, stages)),
            pltpu.SemaphoreType.DMA((parts, stages)),
        ],
        compiler_params=pltpu.CompilerParams(
            collective_id=0, has_side_effects=True, vmem_limit_bytes=60 * 1024 * 1024
        ),
    )(tokens, expert_ids, gate_weights, w_gate, w_up, w_down)


def solution(mesh):
    return jax.shard_map(
        body,
        mesh=mesh,
        in_specs=(
            P(("groups", "expert"), None),
            P(("groups", "expert"), None),
            P(("groups", "expert"), None),
            P("expert", None, None),
            P("expert", None, None),
            P("expert", None, None),
        ),
        out_specs=P(("groups", "expert"), None),
        check_vma=False,
    )
```

```python
import functools

import jax
import jax.numpy as jnp
from jax import lax
from jax.experimental import pallas as pl
from jax.experimental.pallas import tpu as pltpu
from jax.sharding import PartitionSpec as P

EXPERTS = 16
CAP = 8
TILE = 16
LANES = 128
UNITS = 256


def column_spans(size):
    large = -(-size // UNITS) // 2 * UNITS
    if large == 0 or large >= size:
        return [(0, size)]
    return [(0, large), (large, size - large)]


def kernel(
    n,
    tok_hbm,
    ids_ref,
    gw_ref,
    wg_hbm,
    wu_hbm,
    wd_hbm,
    out_ref,
    tok_ref,
    gathered,
    wg,
    wu,
    wd,
    rows_in,
    hidden,
    tail_out,
    kept,
    sending,
    landed,
    tsem,
    wsem,
    dsem,
    ag_send,
    ag_recv,
    rs_send,
    rs_recv,
):
    rows, width = tok_ref.shape
    pad = TILE - rows
    parts = rows // pad
    sec = width // (parts + 1)
    packed = parts * sec
    units = wg.shape[1]
    spans = column_spans(sec)
    descending = [n >> (k + 1) for k in range(n.bit_length() - 1)]
    swapped = list(descending)
    if len(swapped) > 2:
        swapped[-2], swapped[-3] = swapped[-3], swapped[-2]
    slots = n * CAP
    stages = n.bit_length() - 1
    chunks = [(s, u) for u in range(len(spans)) for s in range(parts)]
    me = lax.axis_index("expert")

    def partner(bit):
        return me + bit - 2 * bit * ((me // bit) % 2)

    def weight_copies(j):
        cols = pl.ds(j * UNITS, UNITS)
        return (
            pltpu.make_async_copy(wg_hbm.at[0, :, cols], wg.at[:, cols], wsem.at[0, j]),
            pltpu.make_async_copy(wu_hbm.at[0, :, cols], wu.at[:, cols], wsem.at[1, j]),
        )

    def down_copy(s, u):
        cols = pl.ds(s * sec + spans[u][0], spans[u][1])
        return pltpu.make_async_copy(wd_hbm.at[0, :, cols], wd.at[:, cols], dsem.at[s, u])

    token_copy = pltpu.make_async_copy(tok_hbm, tok_ref, tsem)
    token_copy.start()

    barrier = pltpu.get_barrier_semaphore()
    for k in range(stages):
        pl.semaphore_signal(barrier, inc=1, device_id={"expert": partner(1 << k)})

    for j in range(units // UNITS):
        for copy in weight_copies(j):
            copy.start()
    for u in range(len(spans)):
        for s in [parts] + list(range(parts)):
            down_copy(s, u).start()

    lane = lax.broadcasted_iota(jnp.int32, (rows, LANES), 1)
    row = lax.broadcasted_iota(jnp.int32, (rows, LANES), 0)
    expert_t = lax.broadcasted_iota(jnp.int32, (LANES, rows), 0) % EXPERTS
    weight_t = jnp.zeros((LANES, rows), jnp.float32)
    for j in range(ids_ref.shape[0]):
        weight_t = weight_t + jnp.where(
            ids_ref[j : j + 1, :] == expert_t, gw_ref[j : j + 1, :], 0.0
        )
    weight = weight_t.T
    chosen = jnp.where(weight > 0.0, 1.0, 0.0)
    slot = jnp.zeros((rows, LANES), jnp.float32)
    for t in range(rows - 1):
        slot = slot + jnp.where(row > t, chosen[t : t + 1, :], 0.0)
    first = weight.astype(jnp.bfloat16).astype(jnp.float32)
    second = (weight - first).astype(jnp.bfloat16).astype(jnp.float32)
    third = weight - first - second
    kind = lane // EXPERTS
    route = jnp.where(
        kind == 0,
        slot,
        jnp.where(kind == 1, first, jnp.where(kind == 2, second, jnp.where(kind == 3, third, 0.0))),
    )
    gathered[0:TILE, :LANES] = jnp.concatenate(
        [route, jnp.zeros((pad, LANES), jnp.float32)], axis=0
    ).astype(jnp.bfloat16)
    token_copy.wait()
    mine = tok_ref[...].astype(jnp.float32)
    for s in range(parts):
        gathered[0:TILE, LANES + s * sec : LANES + (s + 1) * sec] = jnp.concatenate(
            [mine[:, s * sec : (s + 1) * sec], mine[pad * s : pad * (s + 1), packed:]], axis=0
        ).astype(jnp.bfloat16)

    pl.semaphore_wait(barrier, stages)

    def position(mask):
        return sum(1 << k for k, bit in enumerate(descending) if mask & bit)

    def order_of(s):
        return swapped if s % 3 == 1 else descending

    def gather_copy(s, mask, bit):
        first_col = 0 if s == 0 else LANES + s * sec
        cols = pl.ds(first_col, LANES + (s + 1) * sec - first_col)
        to = position(mask | bit)
        return pltpu.make_async_remote_copy(
            src_ref=gathered.at[pl.ds(position(mask) * TILE, TILE), cols],
            dst_ref=gathered.at[pl.ds(to * TILE, TILE), cols],
            send_sem=ag_send.at[s, to],
            recv_sem=ag_recv.at[s, to],
            device_id={"expert": partner(bit)},
            device_id_type=pl.DeviceIdType.MESH,
        )

    def came_by(s, mask):
        return [bit for bit in order_of(s) if mask & bit][-1]

    for k in range(stages):
        for s in range(parts):
            gather_copy(s, 0, order_of(s)[k]).start()
    arrivals = [(s, mask) for s in range(parts) for mask in range(1, n)]
    arrivals.sort(key=lambda a: (a[1] & 1, bin(a[1]).count("1"), a[0], -a[1]))
    for s, mask in arrivals:
        bit = came_by(s, mask)
        gather_copy(s, mask - bit, bit).wait_recv()
        bits = order_of(s)
        for later in bits[bits.index(bit) + 1 :]:
            gather_copy(s, mask, later).start()

    expert = me % EXPERTS
    all_rows = n * TILE
    lanes = lax.broadcasted_iota(jnp.int32, (all_rows, LANES), 1)
    table = gathered[:, :LANES].astype(jnp.float32)
    slot_of = jnp.sum(jnp.where(lanes == expert, table, 0.0), axis=1, keepdims=True)
    weight_of = jnp.sum(
        jnp.where((lanes % EXPERTS == expert) & (lanes >= EXPERTS), table, 0.0),
        axis=1,
        keepdims=True,
    )
    r_at = lax.broadcasted_iota(jnp.int32, (all_rows, slots), 0)
    m_at = lax.broadcasted_iota(jnp.int32, (all_rows, slots), 1)
    mixing = jnp.where(
        (r_at // TILE == m_at // CAP) & (slot_of == (m_at % CAP).astype(jnp.float32)),
        weight_of,
        0.0,
    )
    mixing_t = mixing.T
    slot_weight = jnp.sum(mixing_t, axis=1, keepdims=True)
    place = jnp.where(mixing > 0.0, 1.0, 0.0)
    pick = jnp.where(mixing_t > 0.0, 1.0, 0.0)
    spare = r_at % TILE >= rows
    spare_t = lax.broadcasted_iota(jnp.int32, (slots, all_rows), 1) % TILE >= rows
    spot = [
        position(sum(bit for j, bit in enumerate(swapped) if i >> j & 1)) for i in range(n)
    ]
    places = {
        0: place,
        1: jnp.concatenate([place[TILE * i : TILE * (i + 1)] for i in spot], axis=0),
    }
    pick_main = pick.astype(jnp.bfloat16)

    tail = jnp.zeros((slots, sec), jnp.float32)
    for s in range(parts):
        data = gathered[:, LANES + s * sec : LANES + (s + 1) * sec]
        rows_in[:, s * sec : (s + 1) * sec] = jnp.dot(
            pick_main, data, preferred_element_type=jnp.float32
        ).astype(jnp.bfloat16)
        pick_tail = jnp.where(spare_t, pltpu.roll(pick, rows - pad * s, 1), 0.0)
        tail = tail + jnp.dot(
            pick_tail.astype(jnp.bfloat16), data, preferred_element_type=jnp.float32
        )
    rows_in[:, packed:] = tail.astype(jnp.bfloat16)

    @pl.loop(0, units // UNITS)
    def _(j):
        for copy in weight_copies(j):
            copy.wait()
        cols = pl.ds(pl.multiple_of(j * UNITS, UNITS), UNITS)
        gate = jnp.dot(rows_in[...], wg[:, cols], preferred_element_type=jnp.float32)
        up = jnp.dot(rows_in[...], wu[:, cols], preferred_element_type=jnp.float32)
        hidden[:, cols] = (gate / (1.0 + jnp.exp(-gate)) * up).astype(jnp.bfloat16)

    def down(s, u):
        down_copy(s, u).wait()
        at, size = spans[u]
        result = jnp.dot(
            hidden[...],
            wd[:, s * sec + at : s * sec + at + size],
            preferred_element_type=jnp.float32,
        )
        return (result * slot_weight).astype(jnp.bfloat16)

    def sum_copy(c, t):
        s, u = chunks[c]
        half = all_rows >> (t + 1)
        cols = pl.ds(spans[u][0], spans[u][1])
        return pltpu.make_async_remote_copy(
            src_ref=sending.at[s, pl.ds(half, half), cols],
            dst_ref=landed.at[s, pl.ds(half, half), cols],
            send_sem=rs_send.at[c, t],
            recv_sem=rs_recv.at[c, t],
            device_id={"expert": partner(order_of(s)[stages - 1 - t])},
            device_id_type=pl.DeviceIdType.MESH,
        )

    def columns(c):
        s, u = chunks[c]
        return s, slice(spans[u][0], spans[u][0] + spans[u][1])

    def first_stage(c):
        s, u = chunks[c]
        _, cols = columns(c)
        if s == 0:
            tail_out[:, cols] = down(parts, u)
        here = down(s, u)
        spot_of = places[1 if s % 3 == 1 else 0]
        place_tail = jnp.where(spare, pltpu.roll(spot_of, rows - pad * s, 0), 0.0)
        half = all_rows // 2
        total = jnp.dot(
            spot_of.astype(jnp.bfloat16), here, preferred_element_type=jnp.float32
        ) + jnp.dot(
            place_tail.astype(jnp.bfloat16), tail_out[:, cols], preferred_element_type=jnp.float32
        )
        sending[s, half:, cols] = total[half:].astype(jnp.bfloat16)
        sum_copy(c, 0).start()
        kept[s, :, cols] = total[:half]

    def later_stage(c, t):
        s, cols = columns(c)
        sum_copy(c, t - 1).wait_recv()
        half = all_rows >> (t + 1)
        upper = kept[s, half : 2 * half, cols] + landed[s, 3 * half : 4 * half, cols].astype(
            jnp.float32
        )
        sending[s, half : 2 * half, cols] = upper.astype(jnp.bfloat16)
        sum_copy(c, t).start()
        kept[s, :half, cols] = kept[s, :half, cols] + landed[
            s, 2 * half : 3 * half, cols
        ].astype(jnp.float32)

    def last_stage(c):
        s, u = chunks[c]
        _, cols = columns(c)
        sum_copy(c, stages - 1).wait_recv()
        done = kept[s, :TILE, cols] + landed[s, TILE : 2 * TILE, cols].astype(jnp.float32)
        at, size = spans[u]
        out_ref[:, s * sec + at : s * sec + at + size] = done[:rows].astype(jnp.bfloat16)
        tails[u].append(done[rows:])
        if s == parts - 1:
            out_ref[:, packed + at : packed + at + size] = jnp.concatenate(
                tails[u], axis=0
            ).astype(jnp.bfloat16)

    tails = [[] for _ in spans]
    first_stage(0)
    for c in range(1, len(chunks)):
        first_stage(c)
        later_stage(c - 1, 1)
    later_stage(len(chunks) - 1, 1)
    for step in range(len(chunks) + stages):
        for c in range(len(chunks)):
            t = step - c + 2
            if 2 <= t < stages:
                later_stage(c, t)
            elif t == stages:
                last_stage(c)

    for s in range(parts):
        for mask in range(1, n):
            bit = came_by(s, mask)
            gather_copy(s, mask - bit, bit).wait_send()
    for c in range(len(chunks)):
        for t in range(stages):
            sum_copy(c, t).wait_send()


def body(tokens, expert_ids, gate_weights, w_gate, w_up, w_down):
    n = lax.axis_size("expert")
    rows, width = tokens.shape
    units = w_gate.shape[2]
    pad = TILE - rows
    parts = rows // pad
    sec = width // (parts + 1)
    stages = n.bit_length() - 1
    spans = len(column_spans(sec))
    vmem = pl.BlockSpec(memory_space=pltpu.VMEM)
    hbm = pl.BlockSpec(memory_space=pl.ANY)
    return pl.pallas_call(
        functools.partial(kernel, n),
        out_shape=jax.ShapeDtypeStruct((rows, width), jnp.bfloat16),
        in_specs=[hbm, vmem, vmem, hbm, hbm, hbm],
        out_specs=vmem,
        scratch_shapes=[
            pltpu.VMEM((rows, width), jnp.bfloat16),
            pltpu.VMEM((n * TILE, parts * sec + LANES), jnp.bfloat16),
            pltpu.VMEM((width, units), jnp.bfloat16),
            pltpu.VMEM((width, units), jnp.bfloat16),
            pltpu.VMEM((units, width), jnp.bfloat16),
            pltpu.VMEM((n * CAP, width), jnp.bfloat16),
            pltpu.VMEM((n * CAP, units), jnp.bfloat16),
            pltpu.VMEM((n * CAP, sec), jnp.bfloat16),
            pltpu.VMEM((parts, n * TILE // 2, sec), jnp.float32),
            pltpu.VMEM((parts, n * TILE, sec), jnp.bfloat16),
            pltpu.VMEM((parts, n * TILE, sec), jnp.bfloat16),
            pltpu.SemaphoreType.DMA,
            pltpu.SemaphoreType.DMA((2, units // UNITS)),
            pltpu.SemaphoreType.DMA((parts + 1, spans)),
            pltpu.SemaphoreType.DMA((parts, n)),
            pltpu.SemaphoreType.DMA((parts, n)),
            pltpu.SemaphoreType.DMA((parts * spans, stages)),
            pltpu.SemaphoreType.DMA((parts * spans, stages)),
        ],
        compiler_params=pltpu.CompilerParams(
            collective_id=0, has_side_effects=True, vmem_limit_bytes=60 * 1024 * 1024
        ),
    )(tokens, expert_ids.T, gate_weights.T, w_gate, w_up, w_down)


def solution(mesh):
    return jax.shard_map(
        body,
        mesh=mesh,
        in_specs=(
            P(("groups", "expert"), None),
            P(("groups", "expert"), None),
            P(("groups", "expert"), None),
            P("expert", None, None),
            P("expert", None, None),
            P("expert", None, None),
        ),
        out_specs=P(("groups", "expert"), None),
        check_vma=False,
    )
```

```python
import functools

import jax
import jax.numpy as jnp
from jax import lax
from jax.experimental import pallas as pl
from jax.experimental.pallas import tpu as pltpu
from jax.sharding import PartitionSpec as P

EXPERTS = 16
CAP = 8
TILE = 16
LANES = 128
UNITS = 256


def column_spans(size):
    large = -(-size // UNITS) // 2 * UNITS
    if large == 0 or large >= size:
        return [(0, size)]
    return [(0, large), (large, size - large)]


def kernel(
    n,
    tok_hbm,
    ids_ref,
    gw_ref,
    wg_hbm,
    wu_hbm,
    wd_hbm,
    out_ref,
    tok_ref,
    gathered,
    wg,
    wu,
    wd,
    rows_in,
    hidden,
    tail_out,
    kept,
    sending,
    landed,
    tsem,
    wsem,
    dsem,
    ag_send,
    ag_recv,
    rs_send,
    rs_recv,
):
    rows, width = tok_ref.shape
    pad = TILE - rows
    parts = rows // pad
    sec = width // (parts + 1)
    packed = parts * sec
    units = wg.shape[1]
    spans = column_spans(sec)
    descending = [n >> (k + 1) for k in range(n.bit_length() - 1)]
    swapped = list(descending)
    if len(swapped) > 2:
        swapped[-2], swapped[-3] = swapped[-3], swapped[-2]
    slots = n * CAP
    stages = n.bit_length() - 1
    chunks = [(s, u) for u in range(len(spans)) for s in range(parts)]
    me = lax.axis_index("expert")

    def partner(bit):
        return me + bit - 2 * bit * ((me // bit) % 2)

    def weight_copies(j):
        cols = pl.ds(j * UNITS, UNITS)
        return (
            pltpu.make_async_copy(wg_hbm.at[0, :, cols], wg.at[:, cols], wsem.at[0, j]),
            pltpu.make_async_copy(wu_hbm.at[0, :, cols], wu.at[:, cols], wsem.at[1, j]),
        )

    def down_copy(s, u):
        cols = pl.ds(s * sec + spans[u][0], spans[u][1])
        return pltpu.make_async_copy(wd_hbm.at[0, :, cols], wd.at[:, cols], dsem.at[s, u])

    token_copy = pltpu.make_async_copy(tok_hbm, tok_ref, tsem)
    token_copy.start()

    barrier = pltpu.get_barrier_semaphore()
    for k in range(stages):
        pl.semaphore_signal(barrier, inc=1, device_id={"expert": partner(1 << k)})

    for j in range(units // UNITS):
        for copy in weight_copies(j):
            copy.start()
    for u in range(len(spans)):
        for s in [parts] + list(range(parts)):
            down_copy(s, u).start()

    lane = lax.broadcasted_iota(jnp.int32, (rows, LANES), 1)
    row = lax.broadcasted_iota(jnp.int32, (rows, LANES), 0)
    expert_t = lax.broadcasted_iota(jnp.int32, (LANES, rows), 0) % EXPERTS
    weight_t = jnp.zeros((LANES, rows), jnp.float32)
    for j in range(ids_ref.shape[0]):
        weight_t = weight_t + jnp.where(
            ids_ref[j : j + 1, :] == expert_t, gw_ref[j : j + 1, :], 0.0
        )
    weight = weight_t.T
    chosen = jnp.where(weight > 0.0, 1.0, 0.0)
    slot = jnp.zeros((rows, LANES), jnp.float32)
    for t in range(rows - 1):
        slot = slot + jnp.where(row > t, chosen[t : t + 1, :], 0.0)
    first = weight.astype(jnp.bfloat16).astype(jnp.float32)
    second = (weight - first).astype(jnp.bfloat16).astype(jnp.float32)
    third = weight - first - second
    kind = lane // EXPERTS
    route = jnp.where(
        kind == 0,
        slot,
        jnp.where(kind == 1, first, jnp.where(kind == 2, second, jnp.where(kind == 3, third, 0.0))),
    )
    gathered[0][0:TILE, :LANES] = jnp.concatenate(
        [route, jnp.zeros((pad, LANES), jnp.float32)], axis=0
    ).astype(jnp.bfloat16)
    token_copy.wait()
    mine = tok_ref[...].astype(jnp.float32)
    for s in range(parts):
        gathered[s][0:TILE, gathered[s].shape[1] - sec :] = jnp.concatenate(
            [mine[:, s * sec : (s + 1) * sec], mine[pad * s : pad * (s + 1), packed:]], axis=0
        ).astype(jnp.bfloat16)

    pl.semaphore_wait(barrier, stages)

    def position(mask):
        return sum(1 << k for k, bit in enumerate(descending) if mask & bit)

    def order_of(s):
        return swapped if s % 3 == 1 else descending

    def gather_copy(s, mask, bit):
        to = position(mask | bit)
        return pltpu.make_async_remote_copy(
            src_ref=gathered[s].at[pl.ds(position(mask) * TILE, TILE), :],
            dst_ref=gathered[s].at[pl.ds(to * TILE, TILE), :],
            send_sem=ag_send.at[s, to],
            recv_sem=ag_recv.at[s, to],
            device_id={"expert": partner(bit)},
            device_id_type=pl.DeviceIdType.MESH,
        )

    def came_by(s, mask):
        return [bit for bit in order_of(s) if mask & bit][-1]

    for k in range(stages):
        for s in range(parts):
            gather_copy(s, 0, order_of(s)[k]).start()
    arrivals = [(s, mask) for s in range(parts) for mask in range(1, n)]
    arrivals.sort(key=lambda a: (a[1] & 1, bin(a[1]).count("1"), a[0], a[1] & 2, a[1]))
    for s, mask in arrivals:
        bit = came_by(s, mask)
        gather_copy(s, mask - bit, bit).wait_recv()
        bits = order_of(s)
        for later in bits[bits.index(bit) + 1 :]:
            gather_copy(s, mask, later).start()

    expert = me % EXPERTS
    all_rows = n * TILE
    lanes = lax.broadcasted_iota(jnp.int32, (all_rows, LANES), 1)
    table = gathered[0][:, :LANES].astype(jnp.float32)
    slot_of = jnp.sum(jnp.where(lanes == expert, table, 0.0), axis=1, keepdims=True)
    weight_of = jnp.sum(
        jnp.where((lanes % EXPERTS == expert) & (lanes >= EXPERTS), table, 0.0),
        axis=1,
        keepdims=True,
    )
    r_at = lax.broadcasted_iota(jnp.int32, (all_rows, slots), 0)
    m_at = lax.broadcasted_iota(jnp.int32, (all_rows, slots), 1)
    mixing = jnp.where(
        (r_at // TILE == m_at // CAP) & (slot_of == (m_at % CAP).astype(jnp.float32)),
        weight_of,
        0.0,
    )
    mixing_t = mixing.T
    slot_weight = jnp.sum(mixing_t, axis=1, keepdims=True)
    place = jnp.where(mixing > 0.0, 1.0, 0.0)
    pick = jnp.where(mixing_t > 0.0, 1.0, 0.0)
    spare = r_at % TILE >= rows
    spare_t = lax.broadcasted_iota(jnp.int32, (slots, all_rows), 1) % TILE >= rows
    spot = [
        position(sum(bit for j, bit in enumerate(swapped) if i >> j & 1)) for i in range(n)
    ]
    places = {
        0: place,
        1: jnp.concatenate([place[TILE * i : TILE * (i + 1)] for i in spot], axis=0),
    }
    pick_main = pick.astype(jnp.bfloat16)

    tail = jnp.zeros((slots, sec), jnp.float32)
    for s in range(parts):
        data = gathered[s][:, gathered[s].shape[1] - sec :]
        rows_in[:, s * sec : (s + 1) * sec] = jnp.dot(
            pick_main, data, preferred_element_type=jnp.float32
        ).astype(jnp.bfloat16)
        pick_tail = jnp.where(spare_t, pltpu.roll(pick, rows - pad * s, 1), 0.0)
        tail = tail + jnp.dot(
            pick_tail.astype(jnp.bfloat16), data, preferred_element_type=jnp.float32
        )
    rows_in[:, packed:] = tail.astype(jnp.bfloat16)

    @pl.loop(0, units // UNITS)
    def _(j):
        for copy in weight_copies(j):
            copy.wait()
        cols = pl.ds(pl.multiple_of(j * UNITS, UNITS), UNITS)
        gate = jnp.dot(rows_in[...], wg[:, cols], preferred_element_type=jnp.float32)
        up = jnp.dot(rows_in[...], wu[:, cols], preferred_element_type=jnp.float32)
        hidden[:, cols] = (gate / (1.0 + jnp.exp(-gate)) * up).astype(jnp.bfloat16)

    def down(s, u):
        down_copy(s, u).wait()
        at, size = spans[u]
        result = jnp.dot(
            hidden[...],
            wd[:, s * sec + at : s * sec + at + size],
            preferred_element_type=jnp.float32,
        )
        return (result * slot_weight).astype(jnp.bfloat16)

    def sum_copy(c, t):
        s, u = chunks[c]
        half = all_rows >> (t + 1)
        return pltpu.make_async_remote_copy(
            src_ref=sending[u].at[s, pl.ds(half, half), :],
            dst_ref=landed[u].at[s, pl.ds(half, half), :],
            send_sem=rs_send.at[c, t],
            recv_sem=rs_recv.at[c, t],
            device_id={"expert": partner(order_of(s)[stages - 1 - t])},
            device_id_type=pl.DeviceIdType.MESH,
        )

    def columns(c):
        s, u = chunks[c]
        return s, slice(spans[u][0], spans[u][0] + spans[u][1])

    def first_stage(c):
        s, u = chunks[c]
        _, cols = columns(c)
        if s == 0:
            tail_out[:, cols] = down(parts, u)
        here = down(s, u)
        spot_of = places[1 if s % 3 == 1 else 0]
        place_tail = jnp.where(spare, pltpu.roll(spot_of, rows - pad * s, 0), 0.0)
        half = all_rows // 2
        total = jnp.dot(
            spot_of.astype(jnp.bfloat16), here, preferred_element_type=jnp.float32
        ) + jnp.dot(
            place_tail.astype(jnp.bfloat16), tail_out[:, cols], preferred_element_type=jnp.float32
        )
        sending[u][s, half:, :] = total[half:].astype(jnp.bfloat16)
        sum_copy(c, 0).start()
        kept[s, :, cols] = total[:half]

    def later_stage(c, t):
        s, u = chunks[c]
        _, cols = columns(c)
        sum_copy(c, t - 1).wait_recv()
        half = all_rows >> (t + 1)
        upper = kept[s, half : 2 * half, cols] + landed[u][s, 3 * half : 4 * half, :].astype(
            jnp.float32
        )
        sending[u][s, half : 2 * half, :] = upper.astype(jnp.bfloat16)
        sum_copy(c, t).start()
        kept[s, :half, cols] = kept[s, :half, cols] + landed[u][
            s, 2 * half : 3 * half, :
        ].astype(jnp.float32)

    def last_stage(c):
        s, u = chunks[c]
        _, cols = columns(c)
        sum_copy(c, stages - 1).wait_recv()
        done = kept[s, :TILE, cols] + landed[u][s, TILE : 2 * TILE, :].astype(jnp.float32)
        at, size = spans[u]
        out_ref[:, s * sec + at : s * sec + at + size] = done[:rows].astype(jnp.bfloat16)
        tails[u].append(done[rows:])
        if s == parts - 1:
            out_ref[:, packed + at : packed + at + size] = jnp.concatenate(
                tails[u], axis=0
            ).astype(jnp.bfloat16)

    tails = [[] for _ in spans]
    first_stage(0)
    for c in range(1, len(chunks)):
        first_stage(c)
        later_stage(c - 1, 1)
    later_stage(len(chunks) - 1, 1)
    events = [(c + 2.5 * (t - 2), c, t) for c in range(len(chunks)) for t in range(2, stages + 1)]
    for _, c, t in sorted(events):
        if t < stages:
            later_stage(c, t)
        else:
            last_stage(c)

    for s in range(parts):
        for mask in range(1, n):
            bit = came_by(s, mask)
            gather_copy(s, mask - bit, bit).wait_send()
    for c in range(len(chunks)):
        for t in range(stages):
            sum_copy(c, t).wait_send()


def body(tokens, expert_ids, gate_weights, w_gate, w_up, w_down):
    n = lax.axis_size("expert")
    rows, width = tokens.shape
    units = w_gate.shape[2]
    pad = TILE - rows
    parts = rows // pad
    sec = width // (parts + 1)
    stages = n.bit_length() - 1
    spans = column_spans(sec)
    vmem = pl.BlockSpec(memory_space=pltpu.VMEM)
    hbm = pl.BlockSpec(memory_space=pl.ANY)
    return pl.pallas_call(
        functools.partial(kernel, n),
        out_shape=jax.ShapeDtypeStruct((rows, width), jnp.bfloat16),
        in_specs=[hbm, vmem, vmem, hbm, hbm, hbm],
        out_specs=vmem,
        scratch_shapes=[
            pltpu.VMEM((rows, width), jnp.bfloat16),
            [
                pltpu.VMEM((n * TILE, sec + (LANES if s == 0 else 0)), jnp.bfloat16)
                for s in range(parts)
            ],
            pltpu.VMEM((width, units), jnp.bfloat16),
            pltpu.VMEM((width, units), jnp.bfloat16),
            pltpu.VMEM((units, width), jnp.bfloat16),
            pltpu.VMEM((n * CAP, width), jnp.bfloat16),
            pltpu.VMEM((n * CAP, units), jnp.bfloat16),
            pltpu.VMEM((n * CAP, sec), jnp.bfloat16),
            pltpu.VMEM((parts, n * TILE // 2, sec), jnp.float32),
            [pltpu.VMEM((parts, n * TILE, size), jnp.bfloat16) for _, size in spans],
            [pltpu.VMEM((parts, n * TILE, size), jnp.bfloat16) for _, size in spans],
            pltpu.SemaphoreType.DMA,
            pltpu.SemaphoreType.DMA((2, units // UNITS)),
            pltpu.SemaphoreType.DMA((parts + 1, len(spans))),
            pltpu.SemaphoreType.DMA((parts, n)),
            pltpu.SemaphoreType.DMA((parts, n)),
            pltpu.SemaphoreType.DMA((parts * len(spans), stages)),
            pltpu.SemaphoreType.DMA((parts * len(spans), stages)),
        ],
        compiler_params=pltpu.CompilerParams(
            collective_id=0, has_side_effects=True, vmem_limit_bytes=60 * 1024 * 1024
        ),
    )(tokens, expert_ids.T, gate_weights.T, w_gate, w_up, w_down)


def solution(mesh):
    return jax.shard_map(
        body,
        mesh=mesh,
        in_specs=(
            P(("groups", "expert"), None),
            P(("groups", "expert"), None),
            P(("groups", "expert"), None),
            P("expert", None, None),
            P("expert", None, None),
            P("expert", None, None),
        ),
        out_specs=P(("groups", "expert"), None),
        check_vma=False,
    )
```

```python
import functools

import jax
import jax.numpy as jnp
from jax import lax
from jax.experimental import pallas as pl
from jax.experimental.pallas import tpu as pltpu
from jax.sharding import PartitionSpec as P

EXPERTS = 16
CAP = 8
TILE = 16
LANES = 128
UNITS = 256


def column_spans(size):
    large = -(-size // UNITS) // 2 * UNITS
    if large == 0 or large >= size:
        return [(0, size)]
    return [(0, large), (large, size - large)]


def kernel(
    n,
    tok_hbm,
    ids_ref,
    gw_ref,
    wg_hbm,
    wu_hbm,
    wd_hbm,
    out_ref,
    tok_ref,
    gathered,
    wg,
    wu,
    wd,
    rows_in,
    hidden,
    tail_out,
    kept,
    sending,
    landed,
    tsem,
    wsem,
    dsem,
    ag_send,
    ag_recv,
    rs_send,
    rs_recv,
):
    rows, width = tok_ref.shape
    pad = TILE - rows
    parts = rows // pad
    sec = width // (parts + 1)
    packed = parts * sec
    units = wg.shape[1]
    spans = column_spans(sec)
    descending = [n >> (k + 1) for k in range(n.bit_length() - 1)]
    swapped = list(descending)
    if len(swapped) > 2:
        swapped[-2], swapped[-3] = swapped[-3], swapped[-2]
    slots = n * CAP
    stages = n.bit_length() - 1
    chunks = [(s, u) for u in range(len(spans)) for s in range(parts)]
    me = lax.axis_index("expert")

    def partner(bit):
        return me + bit - 2 * bit * ((me // bit) % 2)

    def weight_copies(j):
        cols = pl.ds(j * UNITS, UNITS)
        return (
            pltpu.make_async_copy(wg_hbm.at[0, :, cols], wg.at[:, cols], wsem.at[0, j]),
            pltpu.make_async_copy(wu_hbm.at[0, :, cols], wu.at[:, cols], wsem.at[1, j]),
        )

    def down_copy(s, u):
        cols = pl.ds(s * sec + spans[u][0], spans[u][1])
        return pltpu.make_async_copy(wd_hbm.at[0, :, cols], wd.at[:, cols], dsem.at[s, u])

    token_copy = pltpu.make_async_copy(tok_hbm, tok_ref, tsem)
    token_copy.start()

    barrier = pltpu.get_barrier_semaphore()
    for k in range(stages):
        pl.semaphore_signal(barrier, inc=1, device_id={"expert": partner(1 << k)})

    for j in range(units // UNITS):
        for copy in weight_copies(j):
            copy.start()
    for u in range(len(spans)):
        for s in [parts] + list(range(parts)):
            down_copy(s, u).start()

    lane = lax.broadcasted_iota(jnp.int32, (rows, LANES), 1)
    row = lax.broadcasted_iota(jnp.int32, (rows, LANES), 0)
    expert_t = lax.broadcasted_iota(jnp.int32, (LANES, rows), 0) % EXPERTS
    weight_t = jnp.zeros((LANES, rows), jnp.float32)
    for j in range(ids_ref.shape[0]):
        weight_t = weight_t + jnp.where(
            ids_ref[j : j + 1, :] == expert_t, gw_ref[j : j + 1, :], 0.0
        )
    weight = weight_t.T
    chosen = jnp.where(weight > 0.0, 1.0, 0.0)
    slot = jnp.zeros((rows, LANES), jnp.float32)
    for t in range(rows - 1):
        slot = slot + jnp.where(row > t, chosen[t : t + 1, :], 0.0)
    first = weight.astype(jnp.bfloat16).astype(jnp.float32)
    second = (weight - first).astype(jnp.bfloat16).astype(jnp.float32)
    third = weight - first - second
    kind = lane // EXPERTS
    route = jnp.where(
        kind == 0,
        slot,
        jnp.where(kind == 1, first, jnp.where(kind == 2, second, jnp.where(kind == 3, third, 0.0))),
    )
    gathered[0][0:TILE, :LANES] = jnp.concatenate(
        [route, jnp.zeros((pad, LANES), jnp.float32)], axis=0
    ).astype(jnp.bfloat16)
    token_copy.wait()
    mine = tok_ref[...].astype(jnp.float32)
    for s in range(parts):
        gathered[s][0:TILE, gathered[s].shape[1] - sec :] = jnp.concatenate(
            [mine[:, s * sec : (s + 1) * sec], mine[pad * s : pad * (s + 1), packed:]], axis=0
        ).astype(jnp.bfloat16)

    pl.semaphore_wait(barrier, stages)

    def position(mask):
        return sum(1 << k for k, bit in enumerate(descending) if mask & bit)

    def order_of(s):
        return swapped if s % 3 == 1 else descending

    def gather_copy(s, mask, bit):
        to = position(mask | bit)
        return pltpu.make_async_remote_copy(
            src_ref=gathered[s].at[pl.ds(position(mask) * TILE, TILE), :],
            dst_ref=gathered[s].at[pl.ds(to * TILE, TILE), :],
            send_sem=ag_send.at[s, to],
            recv_sem=ag_recv.at[s, to],
            device_id={"expert": partner(bit)},
            device_id_type=pl.DeviceIdType.MESH,
        )

    def came_by(s, mask):
        return [bit for bit in order_of(s) if mask & bit][-1]

    for k in range(stages):
        for s in range(parts):
            gather_copy(s, 0, order_of(s)[k]).start()
    arrivals = [(s, mask) for s in range(parts) for mask in range(1, n)]
    arrivals.sort(key=lambda a: (a[1] & 1, bin(a[1]).count("1"), a[0], a[1] & 2, a[1]))
    for s, mask in arrivals:
        bit = came_by(s, mask)
        gather_copy(s, mask - bit, bit).wait_recv()
        bits = order_of(s)
        for later in bits[bits.index(bit) + 1 :]:
            gather_copy(s, mask, later).start()

    expert = me % EXPERTS
    all_rows = n * TILE
    lanes = lax.broadcasted_iota(jnp.int32, (all_rows, LANES), 1)
    table = gathered[0][:, :LANES].astype(jnp.float32)
    slot_of = jnp.sum(jnp.where(lanes == expert, table, 0.0), axis=1, keepdims=True)
    weight_of = jnp.sum(
        jnp.where((lanes % EXPERTS == expert) & (lanes >= EXPERTS), table, 0.0),
        axis=1,
        keepdims=True,
    )
    r_at = lax.broadcasted_iota(jnp.int32, (all_rows, slots), 0)
    m_at = lax.broadcasted_iota(jnp.int32, (all_rows, slots), 1)
    mixing = jnp.where(
        (r_at // TILE == m_at // CAP) & (slot_of == (m_at % CAP).astype(jnp.float32)),
        weight_of,
        0.0,
    )
    mixing_t = mixing.T
    slot_weight = jnp.sum(mixing_t, axis=1, keepdims=True)
    place = jnp.where(mixing > 0.0, 1.0, 0.0)
    pick = jnp.where(mixing_t > 0.0, 1.0, 0.0)
    spare = r_at % TILE >= rows
    spare_t = lax.broadcasted_iota(jnp.int32, (slots, all_rows), 1) % TILE >= rows
    spot = [
        position(sum(bit for j, bit in enumerate(swapped) if i >> j & 1)) for i in range(n)
    ]
    places = {
        0: place,
        1: jnp.concatenate([place[TILE * i : TILE * (i + 1)] for i in spot], axis=0),
    }
    pick_main = pick.astype(jnp.bfloat16)

    tail = jnp.zeros((slots, sec), jnp.float32)
    for s in range(parts):
        data = gathered[s][:, gathered[s].shape[1] - sec :]
        rows_in[:, s * sec : (s + 1) * sec] = jnp.dot(
            pick_main, data, preferred_element_type=jnp.float32
        ).astype(jnp.bfloat16)
        pick_tail = jnp.where(spare_t, pltpu.roll(pick, rows - pad * s, 1), 0.0)
        tail = tail + jnp.dot(
            pick_tail.astype(jnp.bfloat16), data, preferred_element_type=jnp.float32
        )
    rows_in[:, packed:] = tail.astype(jnp.bfloat16)

    @pl.loop(0, units // UNITS)
    def _(j):
        for copy in weight_copies(j):
            copy.wait()
        cols = pl.ds(pl.multiple_of(j * UNITS, UNITS), UNITS)
        gate = jnp.dot(rows_in[...], wg[:, cols], preferred_element_type=jnp.float32)
        up = jnp.dot(rows_in[...], wu[:, cols], preferred_element_type=jnp.float32)
        hidden[:, cols] = (gate / (1.0 + jnp.exp(-gate)) * up).astype(jnp.bfloat16)

    def down(s, u):
        down_copy(s, u).wait()
        at, size = spans[u]
        result = jnp.dot(
            hidden[...],
            wd[:, s * sec + at : s * sec + at + size],
            preferred_element_type=jnp.float32,
        )
        return (result * slot_weight).astype(jnp.bfloat16)

    def sum_copy(c, t):
        s, u = chunks[c]
        half = all_rows >> (t + 1)
        return pltpu.make_async_remote_copy(
            src_ref=sending[u].at[s, pl.ds(half, half), :],
            dst_ref=landed[u].at[s, pl.ds(half, half), :],
            send_sem=rs_send.at[c, t],
            recv_sem=rs_recv.at[c, t],
            device_id={"expert": partner(order_of(s)[stages - 1 - t])},
            device_id_type=pl.DeviceIdType.MESH,
        )

    def columns(c):
        s, u = chunks[c]
        return s, slice(spans[u][0], spans[u][0] + spans[u][1])

    def first_stage(c):
        s, u = chunks[c]
        _, cols = columns(c)
        if s == 0:
            tail_out[:, cols] = down(parts, u)
        here = down(s, u)
        spot_of = places[1 if s % 3 == 1 else 0]
        place_tail = jnp.where(spare, pltpu.roll(spot_of, rows - pad * s, 0), 0.0)
        half = all_rows // 2
        total = jnp.dot(
            spot_of.astype(jnp.bfloat16), here, preferred_element_type=jnp.float32
        ) + jnp.dot(
            place_tail.astype(jnp.bfloat16), tail_out[:, cols], preferred_element_type=jnp.float32
        )
        sending[u][s, half:, :] = total[half:].astype(jnp.bfloat16)
        sum_copy(c, 0).start()
        kept[s, :, cols] = total[:half]

    def later_stage(c, t):
        s, u = chunks[c]
        _, cols = columns(c)
        sum_copy(c, t - 1).wait_recv()
        half = all_rows >> (t + 1)
        upper = kept[s, half : 2 * half, cols] + landed[u][s, 3 * half : 4 * half, :].astype(
            jnp.float32
        )
        sending[u][s, half : 2 * half, :] = upper.astype(jnp.bfloat16)
        sum_copy(c, t).start()
        kept[s, :half, cols] = kept[s, :half, cols] + landed[u][
            s, 2 * half : 3 * half, :
        ].astype(jnp.float32)

    def last_stage(c):
        s, u = chunks[c]
        _, cols = columns(c)
        sum_copy(c, stages - 1).wait_recv()
        done = kept[s, :TILE, cols] + landed[u][s, TILE : 2 * TILE, :].astype(jnp.float32)
        at, size = spans[u]
        out_ref[:, s * sec + at : s * sec + at + size] = done[:rows].astype(jnp.bfloat16)
        tails[u].append(done[rows:])
        if s == parts - 1:
            out_ref[:, packed + at : packed + at + size] = jnp.concatenate(
                tails[u], axis=0
            ).astype(jnp.bfloat16)

    tails = [[] for _ in spans]
    first_stage(0)
    for c in range(1, len(chunks)):
        first_stage(c)
        later_stage(c - 1, 1)
    later_stage(len(chunks) - 1, 1)
    events = [(c + 3.5 * (t - 2), c, t) for c in range(len(chunks)) for t in range(2, stages + 1)]
    for _, c, t in sorted(events):
        if t < stages:
            later_stage(c, t)
        else:
            last_stage(c)

    for s in range(parts):
        for mask in range(1, n):
            bit = came_by(s, mask)
            gather_copy(s, mask - bit, bit).wait_send()
    for c in range(len(chunks)):
        for t in range(stages):
            sum_copy(c, t).wait_send()


def body(tokens, expert_ids, gate_weights, w_gate, w_up, w_down):
    n = lax.axis_size("expert")
    rows, width = tokens.shape
    units = w_gate.shape[2]
    pad = TILE - rows
    parts = rows // pad
    sec = width // (parts + 1)
    stages = n.bit_length() - 1
    spans = column_spans(sec)
    vmem = pl.BlockSpec(memory_space=pltpu.VMEM)
    hbm = pl.BlockSpec(memory_space=pl.ANY)
    return pl.pallas_call(
        functools.partial(kernel, n),
        out_shape=jax.ShapeDtypeStruct((rows, width), jnp.bfloat16),
        in_specs=[hbm, vmem, vmem, hbm, hbm, hbm],
        out_specs=vmem,
        scratch_shapes=[
            pltpu.VMEM((rows, width), jnp.bfloat16),
            [
                pltpu.VMEM((n * TILE, sec + (LANES if s == 0 else 0)), jnp.bfloat16)
                for s in range(parts)
            ],
            pltpu.VMEM((width, units), jnp.bfloat16),
            pltpu.VMEM((width, units), jnp.bfloat16),
            pltpu.VMEM((units, width), jnp.bfloat16),
            pltpu.VMEM((n * CAP, width), jnp.bfloat16),
            pltpu.VMEM((n * CAP, units), jnp.bfloat16),
            pltpu.VMEM((n * CAP, sec), jnp.bfloat16),
            pltpu.VMEM((parts, n * TILE // 2, sec), jnp.float32),
            [pltpu.VMEM((parts, n * TILE, size), jnp.bfloat16) for _, size in spans],
            [pltpu.VMEM((parts, n * TILE, size), jnp.bfloat16) for _, size in spans],
            pltpu.SemaphoreType.DMA,
            pltpu.SemaphoreType.DMA((2, units // UNITS)),
            pltpu.SemaphoreType.DMA((parts + 1, len(spans))),
            pltpu.SemaphoreType.DMA((parts, n)),
            pltpu.SemaphoreType.DMA((parts, n)),
            pltpu.SemaphoreType.DMA((parts * len(spans), stages)),
            pltpu.SemaphoreType.DMA((parts * len(spans), stages)),
        ],
        compiler_params=pltpu.CompilerParams(
            collective_id=0, has_side_effects=True, vmem_limit_bytes=60 * 1024 * 1024
        ),
    )(tokens, expert_ids.T, gate_weights.T, w_gate, w_up, w_down)


def solution(mesh):
    return jax.shard_map(
        body,
        mesh=mesh,
        in_specs=(
            P(("groups", "expert"), None),
            P(("groups", "expert"), None),
            P(("groups", "expert"), None),
            P("expert", None, None),
            P("expert", None, None),
            P("expert", None, None),
        ),
        out_specs=P(("groups", "expert"), None),
        check_vma=False,
    )
```
